32 devices in a mesh: row: 8 (over y, x, core), ka: 4 (over z).
Axes of the slice: x: 2, y: 2, z: 4, core: 2. Of those that a mesh axis runs over, the one named last changes fastest.
Arguments:
- pair_rep: bfloat16 [32, 32, 128], P('row', 'ka'), may hold values from -6 to 6
- in_weights: bfloat16 [2, 128, 512], replicated, may hold values from -0.5 to 0.5
- gate_weights: bfloat16 [2, 128, 128], replicated, may hold values from -0.5 to 0.5
- out_weights: bfloat16 [2, 128, 128], replicated, may hold values from -0.5 to 0.5
Outputs:
- refined: bfloat16 [32, 32, 128], P('row', 'ka')
The draws below stay inside these ranges and needn't reach their ends.
All inputs are finite; a program needn't handle non-finite values.
Results may differ from the reference program's by a relative error of at most 0.015.
Values may be sent and summed in bfloat16 or wider, within the bound.
A program may use at most 64 MiB of HBM per device.

```python
import jax
import jax.numpy as jnp
from jax import lax

PAIR_CH = 128
TRI_CH = 128
N = 32


def level_of(key, dims, pieces, least, high):
    def one(axis_at, parts):
        steps = jax.random.uniform(jax.random.fold_in(jax.random.fold_in(key, 6), axis_at), (parts,), jnp.float32, least / len(pieces), high / len(pieces))
        return jnp.repeat(jnp.exp(steps), dims[axis_at] // parts).reshape((-1,) + (1,) * (len(dims) - axis_at - 1))

    factor_of = one(*pieces[0])
    for cut in pieces[1:]:
        factor_of = factor_of * one(*cut)
    return factor_of


def scatter_about(rng, extent, scale, limit, split=(), dtype=jnp.bfloat16):
    factor_of = level_of(rng, extent, split, -0.22, 0.18) if split else 1.0
    array = jax.random.normal(rng, extent, jnp.float32) * scale * factor_of
    return jnp.minimum(jnp.maximum(array, -limit), limit).astype(dtype)


def setup_inputs(seed: int = 0) -> dict:
    keys = jax.random.split(jax.random.key(seed), 5)
    pair_rep = scatter_about(keys[0], (N, N, PAIR_CH), 1.0, 6.0, ((0, 8), (1, 4)))
    in_weights = scatter_about(keys[1], (2, PAIR_CH, 4 * TRI_CH), PAIR_CH ** -0.5, 0.5)
    gate_weights = scatter_about(keys[2], (2, PAIR_CH, PAIR_CH), PAIR_CH ** -0.5, 0.5)
    out_weights = scatter_about(keys[3], (2, TRI_CH, PAIR_CH), TRI_CH ** -0.5, 0.5)
    return {"pair_rep": pair_rep, "in_weights": in_weights, "gate_weights": gate_weights, "out_weights": out_weights}


EPSILON = 1e-05

def layer_norm(values):
    values = values.astype(jnp.float32)
    centre = lax.optimization_barrier(jnp.mean(values, axis=-1, keepdims=True))
    shifted = values - centre
    spread = lax.optimization_barrier(jnp.mean(shifted * shifted, axis=-1, keepdims=True))
    return shifted * jax.lax.rsqrt(spread + EPSILON)

def reference(pair_rep, in_weights, gate_weights, out_weights):
    state = pair_rep
    for section in range(2):
        normed = layer_norm(state).astype(jnp.bfloat16)
        flattened = normed.reshape(-1, PAIR_CH)
        projected = jnp.dot(flattened, in_weights[section], preferred_element_type=jnp.float32)
        left_rows = (jax.nn.sigmoid(projected[:, :TRI_CH]) * projected[:, TRI_CH:2 * TRI_CH]).astype(jnp.bfloat16)
        right_rows = (jax.nn.sigmoid(projected[:, 2 * TRI_CH:3 * TRI_CH]) * projected[:, 3 * TRI_CH:]).astype(jnp.bfloat16)
        left_rows = left_rows.reshape(N, N, TRI_CH)
        right_rows = right_rows.reshape(N, N, TRI_CH)
        gating = jax.nn.sigmoid(jnp.dot(flattened, gate_weights[section], preferred_element_type=jnp.float32))
        gating = gating.reshape(N, N, PAIR_CH)
        if section == 1:
            left_rows = jnp.transpose(left_rows, (1, 0, 2))
            right_rows = jnp.transpose(right_rows, (1, 0, 2))
        product = jnp.einsum('ikh,jkh->ijh', left_rows.astype(jnp.float32), right_rows.astype(jnp.float32))
        squeezed = layer_norm(product).astype(jnp.bfloat16).reshape(-1, TRI_CH)
        update = jnp.dot(squeezed, out_weights[section], preferred_element_type=jnp.float32).reshape(N, N, PAIR_CH)
        state = (state.astype(jnp.float32) + gating * update).astype(jnp.bfloat16)
    return state
```

```python
import functools

import jax
import jax.numpy as jnp
from jax import lax
from jax.experimental import pallas as pl
from jax.experimental.pallas import tpu as pltpu
from jax.sharding import PartitionSpec as P

EPSILON = 1e-05
MESH = pl.DeviceIdType.MESH
VMEM_BUDGET = 32 * 1024 * 1024


def normalize(values):
    values = values.astype(jnp.float32)
    centre = jnp.mean(values, axis=-1, keepdims=True)
    shifted = values - centre
    spread = jnp.mean(shifted * shifted, axis=-1, keepdims=True)
    return shifted * lax.rsqrt(spread + EPSILON)


def flatten_normed(blocks):
    normed = normalize(blocks).astype(jnp.bfloat16)
    return normed.reshape(-1, blocks.shape[-1])


def operands(flattened, weights, shape):
    columns = weights.shape[1] // 4
    projected = jnp.dot(flattened, weights, preferred_element_type=jnp.float32)
    left_rows = (
        jax.nn.sigmoid(projected[:, :columns]) * projected[:, columns : 2 * columns]
    ).astype(jnp.bfloat16)
    right_rows = (
        jax.nn.sigmoid(projected[:, 2 * columns : 3 * columns]) * projected[:, 3 * columns :]
    ).astype(jnp.bfloat16)
    return (
        left_rows.reshape(shape[0], shape[1], columns),
        right_rows.reshape(shape[0], shape[1], columns),
    )


def gates(flattened, weights, shape):
    gating = jax.nn.sigmoid(jnp.dot(flattened, weights, preferred_element_type=jnp.float32))
    return gating.reshape(shape[0], shape[1], weights.shape[1])


def triangle(left_rows, right_rows):
    partial_value = jnp.einsum(
        "ikh,jkh->ijh",
        left_rows,
        lax.all_gather(right_rows, "row", axis=0, tiled=True),
        preferred_element_type=jnp.float32,
    )
    return lax.psum_scatter(
        partial_value.astype(jnp.bfloat16), "ka", scatter_dimension=1, tiled=True
    ).astype(jnp.float32)


def finish(state, gating, product, weights):
    squeezed = normalize(product).astype(jnp.bfloat16).reshape(-1, product.shape[-1])
    update = jnp.dot(squeezed, weights, preferred_element_type=jnp.float32).reshape(gating.shape)
    return (state.astype(jnp.float32) + gating * update).astype(jnp.bfloat16)


def per_device_large(pair_rep, in_weights, gate_weights, out_weights):
    shape = pair_rep.shape
    flattened = flatten_normed(pair_rep)
    left_rows, right_rows = operands(flattened, in_weights[0], shape)
    gating = gates(flattened, gate_weights[0], shape)
    middle = finish(pair_rep, gating, triangle(left_rows, right_rows), out_weights[0])
    arrived = lax.all_to_all(
        jnp.swapaxes(middle, 0, 1), "ka", split_axis=1, concat_axis=0, tiled=True
    )
    arrived = lax.all_to_all(arrived, "row", split_axis=0, concat_axis=1, tiled=True)
    left_far, right_far = operands(flatten_normed(arrived), in_weights[1], arrived.shape)
    gating_far = gates(flatten_normed(middle), gate_weights[1], shape)
    return finish(middle, gating_far, triangle(left_far, right_far), out_weights[1])


def gated(normed, weights):
    half = weights.shape[1] // 2
    projected = jnp.dot(normed, weights, preferred_element_type=jnp.float32)
    rounded = (jax.nn.sigmoid(projected[:, :half]) * projected[:, half:]).astype(jnp.bfloat16)
    return rounded.astype(jnp.float32)


def closing(state, normed, product, gate_w, out_w):
    update = jnp.dot(
        normalize(product).astype(jnp.bfloat16), out_w, preferred_element_type=jnp.float32
    )
    gating = jax.nn.sigmoid(jnp.dot(normed, gate_w, preferred_element_type=jnp.float32))
    return (state.astype(jnp.float32) + gating * update).astype(jnp.bfloat16)


def gather_blocks(R, K, x_ref, full, own_sem, send_sem, recv_sem, fsend_sem, frecv_sem):
    r, c = lax.axis_index("row"), lax.axis_index("ka")
    partner = r + 1 - 2 * lax.rem(r, 2)
    offsets = [(dr, dc) for dr in range(R // 2) for dc in range(K)][1:]
    own = pltpu.make_async_copy(x_ref, full.at[r, c], own_sem)
    own.start()

    def away(dr, dc):
        return lax.rem(r + 2 * dr, R), lax.rem(c + dc, K)

    def back(row, dr, dc):
        return lax.rem(row + R - 2 * dr, R), lax.rem(c + K - dc, K)

    barrier = pltpu.get_barrier_semaphore()
    for dr, dc in offsets:
        pl.semaphore_signal(barrier, inc=1, device_id=away(dr, dc), device_id_type=MESH)
    pl.semaphore_signal(barrier, inc=1, device_id=(partner, c), device_id_type=MESH)
    own.wait()
    pl.semaphore_wait(barrier, len(offsets) + 1)

    def direct(dr, dc, block):
        at = dr * K + dc
        return pltpu.make_async_remote_copy(
            src_ref=full.at[block], dst_ref=full.at[block],
            send_sem=send_sem.at[at], recv_sem=recv_sem.at[at],
            device_id=away(dr, dc), device_id_type=MESH,
        )

    def forward(dr, dc, block):
        at = dr * K + dc
        return pltpu.make_async_remote_copy(
            src_ref=full.at[block], dst_ref=full.at[block],
            send_sem=fsend_sem.at[at], recv_sem=frecv_sem.at[at],
            device_id=(partner, c), device_id_type=MESH,
        )

    sent = [direct(dr, dc, (r, c)) for dr, dc in reversed(offsets)]
    for copy in sent:
        copy.start()
    forwards = [forward(0, 0, (r, c))]
    forwards[0].start()
    for dr, dc in offsets:
        block = back(r, dr, dc)
        direct(dr, dc, block).wait_recv()
        copy = forward(dr, dc, block)
        copy.start()
        forwards.append(copy)
    for dr, dc in [(0, 0)] + offsets:
        forward(dr, dc, back(partner, dr, dc)).wait_recv()
    for copy in sent + forwards:
        copy.wait_send()


def kernel(
    R, K, rows, cols,
    x_ref, iw_hbm, gw_hbm, ow_hbm, o_ref,
    full, iw, gw, ow, norm, left, right, tri, mid, norm1, left1,
    own_sem, w_sem, send_sem, recv_sem, fsend_sem, frecv_sem,
):
    r, c = lax.axis_index("row"), lax.axis_index("ka")
    loads = [
        pltpu.make_async_copy(src, dst, w_sem.at[n])
        for n, (src, dst) in enumerate(((iw_hbm, iw), (gw_hbm, gw), (ow_hbm, ow)))
    ]
    for load in loads:
        load.start()
    gather_blocks(R, K, x_ref, full, own_sem, send_sem, recv_sem, fsend_sem, frecv_sem)
    for load in loads:
        load.wait()
    compute(R, K, rows, cols, r, c, o_ref, full, iw, gw, ow, norm, left, right, tri, mid, norm1, left1)


def compute(R, K, rows, cols, r, c, o_ref, full, iw, gw, ow, norm, left, right, tri, mid, norm1, left1):
    ch = o_ref.shape[-1]
    hidden = ow.shape[1]
    span = cols // rows
    size = rows * cols
    groups = (c, r // span)

    def project(rb, carry):
        normed = normalize(full[rb].reshape(K * size, ch)).astype(jnp.bfloat16)
        norm[rb] = normed.reshape(K, size, ch)
        left[rb] = gated(normed, iw[0, :, : 2 * hidden]).reshape(K, rows, cols, hidden)
        return carry

    lax.fori_loop(0, R, project, 0)
    for g, block in enumerate(groups):
        for part in range(span):
            values = gated(norm[block * span + part].reshape(K * size, ch), iw[0, :, 2 * hidden :])
            for k in range(K):
                at = ((g * K + k) * span + part) * size
                right[at : at + size, :] = values[k * size : (k + 1) * size]

    def outgoing(rb, carry):
        totals = [jnp.zeros((rows, cols, hidden), jnp.float32) for _ in groups]
        for k in range(K):
            for b in range(cols):
                row = left[rb, k, :, b : b + 1, :]
                for g in range(2):
                    other = right[pl.ds((g * K + k) * span * size + b, cols, stride=cols), :]
                    totals[g] = totals[g] + row * other[None]
        for g in range(2):
            tri[g, rb] = totals[g].reshape(size, hidden)
        return carry

    lax.fori_loop(0, R, outgoing, 0)
    for g, block in enumerate(groups):
        state = full[:, block].reshape(R * size, ch)
        normed = norm[:, block].reshape(R * size, ch)
        product = tri[g].reshape(R * size, hidden)
        middle = closing(state, normed, product, gw[0], ow[0])
        again = normalize(middle).astype(jnp.bfloat16)
        if g == 0:
            mid[...] = middle.reshape(R, size, ch)
            norm1[...] = again.reshape(R, size, ch)
            right1 = gated(again, iw[1, :, 2 * hidden :]).reshape(R * rows, cols, hidden)
            right[: R * size, :] = right1.reshape(R * size, hidden)
        else:
            left1[...] = gated(again, iw[1, :, : 2 * hidden])
    first = lax.rem(r, span) * rows
    totals = [jnp.zeros((cols, hidden), jnp.float32) for _ in range(rows)]
    for k in range(R * rows):
        other = right[k * cols : (k + 1) * cols, :]
        for a in range(rows):
            totals[a] = totals[a] + left1[pl.ds(k * cols + first + a, 1), :] * other
    product = jnp.concatenate(totals, axis=0)
    o_ref[...] = closing(mid[r], norm1[r], product, gw[1], ow[1])


def per_device(R, K, pair_rep, in_weights, gate_weights, out_weights):
    rows, cols, ch = pair_rep.shape
    hidden = out_weights.shape[1]
    size = rows * cols
    span = cols // rows
    scratch = [
        pltpu.VMEM((R, K, size, ch), jnp.bfloat16),
        pltpu.VMEM(in_weights.shape, jnp.bfloat16),
        pltpu.VMEM(gate_weights.shape, jnp.bfloat16),
        pltpu.VMEM(out_weights.shape, jnp.bfloat16),
        pltpu.VMEM((R, K, size, ch), jnp.bfloat16),
        pltpu.VMEM((R, K, rows, cols, hidden), jnp.float32),
        pltpu.VMEM((2 * K * span * size, hidden), jnp.float32),
        pltpu.VMEM((2, R, size, hidden), jnp.float32),
        pltpu.VMEM((R, size, ch), jnp.bfloat16),
        pltpu.VMEM((R, size, ch), jnp.bfloat16),
        pltpu.VMEM((R * size, hidden), jnp.float32),
        pltpu.SemaphoreType.DMA,
        pltpu.SemaphoreType.DMA((3,)),
    ] + [pltpu.SemaphoreType.DMA((R // 2 * K,))] * 4
    result = pl.pallas_call(
        functools.partial(kernel, R, K, rows, cols),
        out_shape=jax.ShapeDtypeStruct((size, ch), jnp.bfloat16),
        in_specs=[pl.BlockSpec(memory_space=pl.ANY)] * 4,
        out_specs=pl.BlockSpec(memory_space=pltpu.VMEM),
        scratch_shapes=scratch,
        compiler_params=pltpu.CompilerParams(collective_id=0, has_side_effects=True),
    )(pair_rep.reshape(size, ch), in_weights, gate_weights, out_weights)
    return result.reshape(rows, cols, ch)


def solution(mesh):
    R, K = mesh.shape["row"], mesh.shape["ka"]

    def body(pair_rep, in_weights, gate_weights, out_weights):
        rows, cols, ch = pair_rep.shape
        bytes_held = 8 * R * K * rows * cols * max(ch, out_weights.shape[1])
        small = bytes_held < VMEM_BUDGET and R % 2 == 0 and cols % rows == 0
        whole = R * rows == K * cols and cols % 8 == 0
        if small and whole:
            return per_device(R, K, pair_rep, in_weights, gate_weights, out_weights)
        return per_device_large(pair_rep, in_weights, gate_weights, out_weights)

    in_specs = (P("row", "ka", None), P(), P(), P())
    out_specs = P("row", "ka", None)
    return jax.shard_map(
        body, mesh=mesh, in_specs=in_specs, out_specs=out_specs, check_vma=False
    )
```

```python
import functools

import jax
import jax.numpy as jnp
from jax import lax
from jax.experimental import pallas as pl
from jax.experimental.pallas import tpu as pltpu
from jax.sharding import PartitionSpec as P

EPSILON = 1e-05
MESH = pl.DeviceIdType.MESH
VMEM_BUDGET = 32 * 1024 * 1024


def normalize(values):
    values = values.astype(jnp.float32)
    centre = jnp.mean(values, axis=-1, keepdims=True)
    shifted = values - centre
    spread = jnp.mean(shifted * shifted, axis=-1, keepdims=True)
    return shifted * lax.rsqrt(spread + EPSILON)


def flatten_normed(blocks):
    normed = normalize(blocks).astype(jnp.bfloat16)
    return normed.reshape(-1, blocks.shape[-1])


def operands(flattened, weights, shape):
    columns = weights.shape[1] // 4
    projected = jnp.dot(flattened, weights, preferred_element_type=jnp.float32)
    left_rows = (
        jax.nn.sigmoid(projected[:, :columns]) * projected[:, columns : 2 * columns]
    ).astype(jnp.bfloat16)
    right_rows = (
        jax.nn.sigmoid(projected[:, 2 * columns : 3 * columns]) * projected[:, 3 * columns :]
    ).astype(jnp.bfloat16)
    return (
        left_rows.reshape(shape[0], shape[1], columns),
        right_rows.reshape(shape[0], shape[1], columns),
    )


def gates(flattened, weights, shape):
    gating = jax.nn.sigmoid(jnp.dot(flattened, weights, preferred_element_type=jnp.float32))
    return gating.reshape(shape[0], shape[1], weights.shape[1])


def triangle(left_rows, right_rows):
    partial_value = jnp.einsum(
        "ikh,jkh->ijh",
        left_rows,
        lax.all_gather(right_rows, "row", axis=0, tiled=True),
        preferred_element_type=jnp.float32,
    )
    return lax.psum_scatter(
        partial_value.astype(jnp.bfloat16), "ka", scatter_dimension=1, tiled=True
    ).astype(jnp.float32)


def finish(state, gating, product, weights):
    squeezed = normalize(product).astype(jnp.bfloat16).reshape(-1, product.shape[-1])
    update = jnp.dot(squeezed, weights, preferred_element_type=jnp.float32).reshape(gating.shape)
    return (state.astype(jnp.float32) + gating * update).astype(jnp.bfloat16)


def per_device_large(pair_rep, in_weights, gate_weights, out_weights):
    shape = pair_rep.shape
    flattened = flatten_normed(pair_rep)
    left_rows, right_rows = operands(flattened, in_weights[0], shape)
    gating = gates(flattened, gate_weights[0], shape)
    middle = finish(pair_rep, gating, triangle(left_rows, right_rows), out_weights[0])
    arrived = lax.all_to_all(
        jnp.swapaxes(middle, 0, 1), "ka", split_axis=1, concat_axis=0, tiled=True
    )
    arrived = lax.all_to_all(arrived, "row", split_axis=0, concat_axis=1, tiled=True)
    left_far, right_far = operands(flatten_normed(arrived), in_weights[1], arrived.shape)
    gating_far = gates(flatten_normed(middle), gate_weights[1], shape)
    return finish(middle, gating_far, triangle(left_far, right_far), out_weights[1])


def gated(normed, weights):
    half = weights.shape[1] // 2
    projected = jnp.dot(normed, weights, preferred_element_type=jnp.float32)
    rounded = (jax.nn.sigmoid(projected[:, :half]) * projected[:, half:]).astype(jnp.bfloat16)
    return rounded.astype(jnp.float32)


def closing(state, normed, product, gate_w, out_w):
    update = jnp.dot(
        normalize(product).astype(jnp.bfloat16), out_w, preferred_element_type=jnp.float32
    )
    gating = jax.nn.sigmoid(jnp.dot(normed, gate_w, preferred_element_type=jnp.float32))
    return (state.astype(jnp.float32) + gating * update).astype(jnp.bfloat16)


def kernel(
    R, K, rows, cols,
    x_ref, iw_hbm, gw_hbm, ow_hbm, o_ref,
    full, iw, gw, ow, norm, left, right, turned, tri, mid, norm1, left1,
    own_sem, w_sem, dsend, drecv, fsend, frecv,
):
    r, c = lax.axis_index("row"), lax.axis_index("ka")
    partner = r + 1 - 2 * lax.rem(r, 2)
    H = R // 2
    own = pltpu.make_async_copy(x_ref, full.at[r, c], own_sem)
    own.start()
    loads = [
        pltpu.make_async_copy(src, dst, w_sem.at[n])
        for n, (src, dst) in enumerate(((iw_hbm, iw), (gw_hbm, gw), (ow_hbm, ow)))
    ]
    for load in loads:
        load.start()

    def ahead(dr, dc):
        return lax.rem(r + 2 * dr, R), lax.rem(c + dc, K)

    def behind(row, dr, dc):
        return lax.rem(row + R - 2 * dr, R), lax.rem(c + K - dc, K)

    barrier = pltpu.get_barrier_semaphore()
    offsets = [(dr, dc) for dr in range(H) for dc in range(K)]
    for dr, dc in offsets[1:]:
        pl.semaphore_signal(barrier, inc=1, device_id=ahead(dr, dc), device_id_type=MESH)
    pl.semaphore_signal(barrier, inc=1, device_id=(partner, c), device_id_type=MESH)
    own.wait()
    pl.semaphore_wait(barrier, len(offsets))

    def remote(block, device, send, recv):
        return pltpu.make_async_remote_copy(
            src_ref=full.at[block], dst_ref=full.at[block], send_sem=send, recv_sem=recv,
            device_id=device, device_id_type=MESH,
        )

    def direct(dr, dc, block):
        return remote(block, ahead(dr, dc), dsend.at[dr, dc], drecv.at[dr, dc])

    def to_partner(dr, dc, block):
        return remote(block, (partner, c), fsend.at[dr, dc], frecv.at[dr, dc])

    sent = []

    def start(copy):
        copy.start()
        sent.append(copy)

    def project(rb):
        normed = normalize(full[rb].reshape(K * rows * cols, full.shape[-1])).astype(jnp.bfloat16)
        norm[rb] = normed.reshape(norm.shape[1:])
        left[rb] = gated(normed, iw[0, :, : 2 * ow.shape[1]]).reshape(left.shape[1:])

    for dr, dc in offsets[1:]:
        start(direct(dr, dc, (r, c)))
    start(to_partner(0, 0, (r, c)))
    for load in loads:
        load.wait()
    for dr, dc in offsets[1:]:
        block = behind(r, dr, dc)
        direct(dr, dc, block).wait_recv()
        start(to_partner(dr, dc, block))
    for dr in range(H):
        project(behind(r, dr, 0)[0])
    for dr, dc in offsets:
        to_partner(dr, dc, behind(partner, dr, dc)).wait_recv()
    for dr in range(H):
        project(behind(partner, dr, 0)[0])
    for copy in sent:
        copy.wait_send()
    compute(R, K, rows, cols, r, c, o_ref, full, iw, gw, ow, norm, left, right, turned, tri, mid, norm1, left1)


def compute(R, K, rows, cols, r, c, o_ref, full, iw, gw, ow, norm, left, right, turned, tri, mid, norm1, left1):
    ch = o_ref.shape[-1]
    hidden = ow.shape[1]
    span = cols // rows
    size = rows * cols
    groups = (c, r // span)

    for g, block in enumerate(groups):
        for part in range(span):
            values = gated(norm[block * span + part].reshape(K * size, ch), iw[0, :, 2 * hidden :])
            for k in range(K):
                at = ((g * K + k) * span + part) * size
                right[at : at + size, :] = values[k * size : (k + 1) * size]

    for g in range(2):
        for k in range(K):
            for b in range(cols):
                at = (g * K + k) * span * size + b
                turned[g, k * cols + b] = right[pl.ds(at, cols, stride=cols), :]

    def outgoing(rb, carry):
        totals = [jnp.zeros((rows, cols, hidden), jnp.float32) for _ in groups]
        for k in range(K):
            for b in range(cols):
                row = left[rb, k, :, b : b + 1, :]
                for g in range(2):
                    totals[g] = totals[g] + row * turned[g, k * cols + b][None]
        for g in range(2):
            tri[g, rb] = totals[g].reshape(size, hidden)
        return carry

    lax.fori_loop(0, R, outgoing, 0, unroll=2)
    for g, block in enumerate(groups):
        state = full[:, block].reshape(R * size, ch)
        normed = norm[:, block].reshape(R * size, ch)
        product = tri[g].reshape(R * size, hidden)
        middle = closing(state, normed, product, gw[0], ow[0])
        again = normalize(middle).astype(jnp.bfloat16)
        if g == 0:
            mid[...] = middle.reshape(R, size, ch)
            norm1[...] = again.reshape(R, size, ch)
            right1 = gated(again, iw[1, :, 2 * hidden :]).reshape(R * rows, cols, hidden)
            right[: R * size, :] = right1.reshape(R * size, hidden)
        else:
            left1[...] = gated(again, iw[1, :, : 2 * hidden])
    first = lax.rem(r, span) * rows
    totals = [jnp.zeros((cols, hidden), jnp.float32) for _ in range(rows)]
    for k in range(R * rows):
        other = right[k * cols : (k + 1) * cols, :]
        for a in range(rows):
            totals[a] = totals[a] + left1[pl.ds(k * cols + first + a, 1), :] * other
    product = jnp.concatenate(totals, axis=0)
    o_ref[...] = closing(mid[r], norm1[r], product, gw[1], ow[1])


def per_device(R, K, pair_rep, in_weights, gate_weights, out_weights):
    rows, cols, ch = pair_rep.shape
    hidden = out_weights.shape[1]
    size = rows * cols
    span = cols // rows
    scratch = [
        pltpu.VMEM((R, K, size, ch), jnp.bfloat16),
        pltpu.VMEM(in_weights.shape, jnp.bfloat16),
        pltpu.VMEM(gate_weights.shape, jnp.bfloat16),
        pltpu.VMEM(out_weights.shape, jnp.bfloat16),
        pltpu.VMEM((R, K, size, ch), jnp.bfloat16),
        pltpu.VMEM((R, K, rows, cols, hidden), jnp.float32),
        pltpu.VMEM((2 * K * span * size, hidden), jnp.float32),
        pltpu.VMEM((2, K * cols, cols, hidden), jnp.float32),
        pltpu.VMEM((2, R, size, hidden), jnp.float32),
        pltpu.VMEM((R, size, ch), jnp.bfloat16),
        pltpu.VMEM((R, size, ch), jnp.bfloat16),
        pltpu.VMEM((R * size, hidden), jnp.float32),
        pltpu.SemaphoreType.DMA,
        pltpu.SemaphoreType.DMA((3,)),
    ] + [pltpu.SemaphoreType.DMA((R // 2, K))] * 4
    result = pl.pallas_call(
        functools.partial(kernel, R, K, rows, cols),
        out_shape=jax.ShapeDtypeStruct((size, ch), jnp.bfloat16),
        in_specs=[pl.BlockSpec(memory_space=pl.ANY)] * 4,
        out_specs=pl.BlockSpec(memory_space=pltpu.VMEM),
        scratch_shapes=scratch,
        compiler_params=pltpu.CompilerParams(collective_id=0, has_side_effects=True),
    )(pair_rep.reshape(size, ch), in_weights, gate_weights, out_weights)
    return result.reshape(rows, cols, ch)


def solution(mesh):
    R, K = mesh.shape["row"], mesh.shape["ka"]

    def body(pair_rep, in_weights, gate_weights, out_weights):
        rows, cols, ch = pair_rep.shape
        bytes_held = 8 * R * K * rows * cols * max(ch, out_weights.shape[1])
        small = bytes_held < VMEM_BUDGET and R % 2 == 0 and cols % rows == 0
        whole = R * rows == K * cols and cols % 8 == 0
        if small and whole:
            return per_device(R, K, pair_rep, in_weights, gate_weights, out_weights)
        return per_device_large(pair_rep, in_weights, gate_weights, out_weights)

    in_specs = (P("row", "ka", None), P(), P(), P())
    out_specs = P("row", "ka", None)
    return jax.shard_map(
        body, mesh=mesh, in_specs=in_specs, out_specs=out_specs, check_vma=False
    )
```

```python
import functools

import jax
import jax.numpy as jnp
from jax import lax
from jax.experimental import pallas as pl
from jax.experimental.pallas import tpu as pltpu
from jax.sharding import PartitionSpec as P

EPSILON = 1e-05
MESH = pl.DeviceIdType.MESH
VMEM_BUDGET = 32 * 1024 * 1024


def normalize(values):
    values = values.astype(jnp.float32)
    centre = jnp.mean(values, axis=-1, keepdims=True)
    shifted = values - centre
    spread = jnp.mean(shifted * shifted, axis=-1, keepdims=True)
    return shifted * lax.rsqrt(spread + EPSILON)


def flatten_normed(blocks):
    normed = normalize(blocks).astype(jnp.bfloat16)
    return normed.reshape(-1, blocks.shape[-1])


def operands(flattened, weights, shape):
    columns = weights.shape[1] // 4
    projected = jnp.dot(flattened, weights, preferred_element_type=jnp.float32)
    left_rows = (
        jax.nn.sigmoid(projected[:, :columns]) * projected[:, columns : 2 * columns]
    ).astype(jnp.bfloat16)
    right_rows = (
        jax.nn.sigmoid(projected[:, 2 * columns : 3 * columns]) * projected[:, 3 * columns :]
    ).astype(jnp.bfloat16)
    return (
        left_rows.reshape(shape[0], shape[1], columns),
        right_rows.reshape(shape[0], shape[1], columns),
    )


def gates(flattened, weights, shape):
    gating = jax.nn.sigmoid(jnp.dot(flattened, weights, preferred_element_type=jnp.float32))
    return gating.reshape(shape[0], shape[1], weights.shape[1])


def triangle(left_rows, right_rows):
    partial_value = jnp.einsum(
        "ikh,jkh->ijh",
        left_rows,
        lax.all_gather(right_rows, "row", axis=0, tiled=True),
        preferred_element_type=jnp.float32,
    )
    return lax.psum_scatter(
        partial_value.astype(jnp.bfloat16), "ka", scatter_dimension=1, tiled=True
    ).astype(jnp.float32)


def finish(state, gating, product, weights):
    squeezed = normalize(product).astype(jnp.bfloat16).reshape(-1, product.shape[-1])
    update = jnp.dot(squeezed, weights, preferred_element_type=jnp.float32).reshape(gating.shape)
    return (state.astype(jnp.float32) + gating * update).astype(jnp.bfloat16)


def per_device_large(pair_rep, in_weights, gate_weights, out_weights):
    shape = pair_rep.shape
    flattened = flatten_normed(pair_rep)
    left_rows, right_rows = operands(flattened, in_weights[0], shape)
    gating = gates(flattened, gate_weights[0], shape)
    middle = finish(pair_rep, gating, triangle(left_rows, right_rows), out_weights[0])
    arrived = lax.all_to_all(
        jnp.swapaxes(middle, 0, 1), "ka", split_axis=1, concat_axis=0, tiled=True
    )
    arrived = lax.all_to_all(arrived, "row", split_axis=0, concat_axis=1, tiled=True)
    left_far, right_far = operands(flatten_normed(arrived), in_weights[1], arrived.shape)
    gating_far = gates(flatten_normed(middle), gate_weights[1], shape)
    return finish(middle, gating_far, triangle(left_far, right_far), out_weights[1])


def gated(normed, weights):
    half = weights.shape[1] // 2
    projected = jnp.dot(normed, weights, preferred_element_type=jnp.float32)
    rounded = (jax.nn.sigmoid(projected[:, :half]) * projected[:, half:]).astype(jnp.bfloat16)
    return rounded.astype(jnp.float32)


def closing(state, normed, product, gate_w, out_w):
    update = jnp.dot(
        normalize(product).astype(jnp.bfloat16), out_w, preferred_element_type=jnp.float32
    )
    gating = jax.nn.sigmoid(jnp.dot(normed, gate_w, preferred_element_type=jnp.float32))
    return (state.astype(jnp.float32) + gating * update).astype(jnp.bfloat16)


def kernel(
    R, K, rows, cols,
    x_ref, iw_hbm, gw_hbm, ow_hbm, o_ref,
    full, iw, gw, ow, norm, left, right, turned, tri, mid, norm1, left1,
    own_sem, w_sem, dsend, drecv, fsend, frecv,
):
    r, c = lax.axis_index("row"), lax.axis_index("ka")
    partner = r + 1 - 2 * lax.rem(r, 2)
    H = R // 2
    own = pltpu.make_async_copy(x_ref, full.at[r, c], own_sem)
    own.start()
    loads = [
        pltpu.make_async_copy(src, dst, w_sem.at[n])
        for n, (src, dst) in enumerate(((iw_hbm, iw), (gw_hbm, gw), (ow_hbm, ow)))
    ]
    for load in loads:
        load.start()

    def ahead(dr, dc):
        return lax.rem(r + 2 * dr, R), lax.rem(c + dc, K)

    def behind(row, dr, dc):
        return lax.rem(row + R - 2 * dr, R), lax.rem(c + K - dc, K)

    barrier = pltpu.get_barrier_semaphore()
    offsets = [(dr, dc) for dr in range(H) for dc in range(K)]
    for dr, dc in offsets[1:]:
        pl.semaphore_signal(barrier, inc=1, device_id=ahead(dr, dc), device_id_type=MESH)
    pl.semaphore_signal(barrier, inc=1, device_id=(partner, c), device_id_type=MESH)
    own.wait()
    pl.semaphore_wait(barrier, len(offsets))

    def remote(block, device, send, recv):
        return pltpu.make_async_remote_copy(
            src_ref=full.at[block], dst_ref=full.at[block], send_sem=send, recv_sem=recv,
            device_id=device, device_id_type=MESH,
        )

    def direct(dr, dc, block):
        return remote(block, ahead(dr, dc), dsend.at[dr, dc], drecv.at[dr, dc])

    def to_partner(dr, dc, block):
        return remote(block, (partner, c), fsend.at[dr, dc], frecv.at[dr, dc])

    sent = []

    def start(copy):
        copy.start()
        sent.append(copy)

    def project(rb):
        normed = normalize(full[rb].reshape(K * rows * cols, full.shape[-1])).astype(jnp.bfloat16)
        norm[rb] = normed.reshape(norm.shape[1:])
        left[rb] = gated(normed, iw[0, :, : 2 * ow.shape[1]]).reshape(left.shape[1:])

    for dr, dc in offsets[1:]:
        start(direct(dr, dc, (r, c)))
    start(to_partner(0, 0, (r, c)))
    for load in loads:
        load.wait()
    for dr, dc in offsets[1:]:
        block = behind(r, dr, dc)
        direct(dr, dc, block).wait_recv()
        start(to_partner(dr, dc, block))
    for dr in range(H):
        project(behind(r, dr, 0)[0])
    for dr, dc in offsets:
        to_partner(dr, dc, behind(partner, dr, dc)).wait_recv()
    for dr in range(H):
        project(behind(partner, dr, 0)[0])
    compute(R, K, rows, cols, r, c, o_ref, full, iw, gw, ow, norm, left, right, turned, tri, mid, norm1, left1)
    for copy in sent:
        copy.wait_send()


def compute(R, K, rows, cols, r, c, o_ref, full, iw, gw, ow, norm, left, right, turned, tri, mid, norm1, left1):
    ch = o_ref.shape[-1]
    hidden = ow.shape[1]
    span = cols // rows
    size = rows * cols
    groups = (c, r // span)

    for g, block in enumerate(groups):
        for part in range(span):
            values = gated(norm[block * span + part].reshape(K * size, ch), iw[0, :, 2 * hidden :])
            for k in range(K):
                at = ((g * K + k) * span + part) * size
                right[at : at + size, :] = values[k * size : (k + 1) * size]

    for g in range(2):
        for k in range(K):
            for b in range(cols):
                at = (g * K + k) * span * size + b
                turned[g, k * cols + b] = right[pl.ds(at, cols, stride=cols), :]

    def outgoing(rb, carry):
        totals = [jnp.zeros((rows, cols, hidden), jnp.float32) for _ in groups]
        for k in range(K):
            for b in range(cols):
                row = left[rb, k, :, b : b + 1, :]
                for g in range(2):
                    totals[g] = totals[g] + row * turned[g, k * cols + b][None]
        for g in range(2):
            tri[g, rb] = totals[g].reshape(size, hidden)
        return carry

    lax.fori_loop(0, R, outgoing, 0, unroll=2)
    for g, block in enumerate(groups):
        state = full[:, block].reshape(R * size, ch)
        normed = norm[:, block].reshape(R * size, ch)
        product = tri[g].reshape(R * size, hidden)
        middle = closing(state, normed, product, gw[0], ow[0])
        again = normalize(middle).astype(jnp.bfloat16)
        if g == 0:
            mid[...] = middle.reshape(R, size, ch)
            norm1[...] = again.reshape(R, size, ch)
            right1 = gated(again, iw[1, :, 2 * hidden :]).reshape(R * rows, cols, hidden)
            right[: R * size, :] = right1.reshape(R * size, hidden)
        else:
            left1[...] = gated(again, iw[1, :, : 2 * hidden])
    first = lax.rem(r, span) * rows
    totals = [jnp.zeros((cols, hidden), jnp.float32) for _ in range(rows)]
    for k in range(R * rows):
        other = right[k * cols : (k + 1) * cols, :]
        for a in range(rows):
            totals[a] = totals[a] + left1[pl.ds(k * cols + first + a, 1), :] * other
    product = jnp.concatenate(totals, axis=0)
    o_ref[...] = closing(mid[r], norm1[r], product, gw[1], ow[1])


def per_device(R, K, pair_rep, in_weights, gate_weights, out_weights):
    rows, cols, ch = pair_rep.shape
    hidden = out_weights.shape[1]
    size = rows * cols
    span = cols // rows
    scratch = [
        pltpu.VMEM((R, K, size, ch), jnp.bfloat16),
        pltpu.VMEM(in_weights.shape, jnp.bfloat16),
        pltpu.VMEM(gate_weights.shape, jnp.bfloat16),
        pltpu.VMEM(out_weights.shape, jnp.bfloat16),
        pltpu.VMEM((R, K, size, ch), jnp.bfloat16),
        pltpu.VMEM((R, K, rows, cols, hidden), jnp.float32),
        pltpu.VMEM((2 * K * span * size, hidden), jnp.float32),
        pltpu.VMEM((2, K * cols, cols, hidden), jnp.float32),
        pltpu.VMEM((2, R, size, hidden), jnp.float32),
        pltpu.VMEM((R, size, ch), jnp.bfloat16),
        pltpu.VMEM((R, size, ch), jnp.bfloat16),
        pltpu.VMEM((R * size, hidden), jnp.float32),
        pltpu.SemaphoreType.DMA,
        pltpu.SemaphoreType.DMA((3,)),
    ] + [pltpu.SemaphoreType.DMA((R // 2, K))] * 4
    result = pl.pallas_call(
        functools.partial(kernel, R, K, rows, cols),
        out_shape=jax.ShapeDtypeStruct((size, ch), jnp.bfloat16),
        in_specs=[pl.BlockSpec(memory_space=pl.ANY)] * 4,
        out_specs=pl.BlockSpec(memory_space=pltpu.VMEM),
        scratch_shapes=scratch,
        compiler_params=pltpu.CompilerParams(collective_id=0, has_side_effects=True, vmem_limit_bytes=56542968),
    )(pair_rep.reshape(size, ch), in_weights, gate_weights, out_weights)
    return result.reshape(rows, cols, ch)


def solution(mesh):
    R, K = mesh.shape["row"], mesh.shape["ka"]

    def body(pair_rep, in_weights, gate_weights, out_weights):
        rows, cols, ch = pair_rep.shape
        bytes_held = 8 * R * K * rows * cols * max(ch, out_weights.shape[1])
        small = bytes_held < VMEM_BUDGET and R % 2 == 0 and cols % rows == 0
        whole = R * rows == K * cols and cols % 8 == 0
        if small and whole:
            return per_device(R, K, pair_rep, in_weights, gate_weights, out_weights)
        return per_device_large(pair_rep, in_weights, gate_weights, out_weights)

    in_specs = (P("row", "ka", None), P(), P(), P())
    out_specs = P("row", "ka", None)
    return jax.shard_map(
        body, mesh=mesh, in_specs=in_specs, out_specs=out_specs, check_vma=False
    )
```
